32 devices in a mesh: row: 8 (over y, x, core), rep: 4 (over z).
Axes of the slice: x: 2, y: 2, z: 4, core: 2. Of those that a mesh axis runs over, the one named last changes fastest.
Arguments:
- features: float32 [16384, 256], P('row'), may hold values from -6 to 6
- adjacency_tiles: float32 [8, 4, 256, 128, 128], P('row', 'rep'), may hold values from -0.25 to 0.25
- tile_rows: int32 [8, 4, 256], P('row', 'rep'), may hold values from 0 to 15, as said below
- tile_cols: int32 [8, 4, 256], P('row', 'rep'), may hold values from 0 to 31, as said below
- tile_counts: int32 [8, 4], P('row', 'rep'), may hold values from 32 to 256, as said below
- plan: int32 [4, 2], replicated, may hold values from 0 to 7, as said below
- weights: float32 [2, 256, 256], replicated, may hold values from -0.375 to 0.375
Outputs:
- embedded: float32 [16384, 256], P(('row', 'rep'))
The draws below stay inside these ranges and needn't reach their ends.
Inputs may be any that keep to these rules, and one draw needn't show every extreme that they name: Within one block row and replica the listed positions (tile_rows, tile_cols) are distinct. Within one block row and replica the listed positions (tile_rows, tile_cols) are distinct. `tile_counts`: some block row and replica lists exactly 256 tiles. `plan`: every block row 0 to 7 appears exactly once in the table.
All inputs are finite; a program needn't handle non-finite values.
Results may differ from the reference program's by a relative error of at most 0.0003.
Values sent between devices are 32-bit elements; how exact they have to be, the bound alone decides.
No kernel may reach another device: no remote copies, remote signals or barrier semaphores. Data moves between devices by JAX's collectives and lax.ppermute only.
A program may use at most 128 MiB of HBM per device.

```python
import jax
import jax.numpy as jnp
from jax import lax

F = 256
TILE = 128
LAYERS = 2
VB = 2048
SECTIONS = 2
TMAX = 256
NV = 16384
N_ROW = 8
N_REP = 4


def tile_positions(key):
    row_tiles = VB // TILE
    position_count = SECTIONS * row_tiles * row_tiles
    device_keys = jax.random.split(jax.random.fold_in(key, 17), N_ROW * N_REP)

    def pick_one(device_key):
        return jax.random.permutation(device_key, position_count)[:TMAX]
    chosen = jax.vmap(pick_one)(device_keys).reshape(N_ROW, N_REP, TMAX).astype(jnp.int32)
    return (chosen % row_tiles, chosen // row_tiles)


def draw_tile_rows(key, part):
    return tile_positions(key)[0]


def draw_tile_cols(key, part):
    return tile_positions(key)[1]


def draw_tile_counts(key, part):
    factors = jax.random.randint(jax.random.fold_in(key, 31), (3, N_ROW, N_REP), 0, 9)
    combined = factors[0] * factors[1] * factors[2]
    lowest = TMAX // 8
    counted = lowest + (TMAX - lowest) * combined // 512
    flat_counts = counted.reshape(N_ROW * N_REP)
    picked = jax.random.randint(jax.random.fold_in(key, 37), (), 0, N_ROW * N_REP)
    positions = jnp.arange(N_ROW * N_REP, dtype=jnp.int32)
    flat_counts = jnp.where(positions == picked, TMAX, flat_counts)
    return flat_counts.reshape(N_ROW, N_REP).astype(jnp.int32)


def draw_plan(key, part):
    order_ids = jax.random.permutation(jax.random.fold_in(key, 23), N_ROW)
    return order_ids.reshape(N_REP, SECTIONS).astype(jnp.int32)


def block_levels(own_key, dims, cuts, low, high):
    def one(axis_at, shards_of):
        heights = jax.random.uniform(jax.random.fold_in(jax.random.fold_in(own_key, 6), axis_at), (shards_of,), jnp.float32, low / len(cuts), high / len(cuts))
        return jnp.repeat(jnp.exp(heights), dims[axis_at] // shards_of).reshape((-1,) + (1,) * (len(dims) - axis_at - 1))

    factor_of = one(*cuts[0])
    for cut in cuts[1:]:
        factor_of = factor_of * one(*cut)
    return factor_of


def gaussian(rng, dims, width, most, cuts=(), held_as=jnp.bfloat16):
    result = width * jax.random.normal(rng, dims, jnp.float32)
    if cuts:
        result = result * block_levels(rng, dims, cuts, -0.22, 0.18)
    return jnp.clip(result, -most, most).astype(held_as)


def setup_inputs(seed: int = 0) -> dict:
    streams_of = jax.random.split(jax.random.key(seed), 8)
    return {
        "features": gaussian(streams_of[0], (NV, F), 1.0, 6.0, ((0, 8),), jnp.float32),
        "adjacency_tiles": gaussian(streams_of[1], (N_ROW, N_REP, TMAX, TILE, TILE), (TILE * TMAX // (4 * (VB // TILE))) ** -0.5, 0.25, ((0, 8), (1, 4)), jnp.float32),
        "tile_rows": draw_tile_rows(jax.random.fold_in(streams_of[7], 71), 0),
        "tile_cols": draw_tile_cols(jax.random.fold_in(streams_of[7], 71), 0),
        "tile_counts": draw_tile_counts(jax.random.fold_in(streams_of[7], 71), 0),
        "plan": draw_plan(jax.random.fold_in(streams_of[7], 71), 0),
        "weights": gaussian(streams_of[6], (LAYERS, F, F), F ** -0.5, 0.375, (), jnp.float32),
    }


def spread(hidden, adjacency_tiles, tile_rows, tile_cols, tile_counts, plan):
    row_tiles = VB // TILE
    pieces = hidden.reshape(N_ROW * row_tiles, TILE, F)
    slot_ids = jnp.arange(TMAX, dtype=jnp.int32)
    lane_ids = jnp.arange(row_tiles, dtype=jnp.int32)

    def one_row(row_num):
        def one_rep(running, rep_num):
            column_ids = tile_cols[row_num, rep_num]
            owner_ids = plan[rep_num][column_ids // row_tiles]
            picked = (owner_ids * row_tiles + column_ids % row_tiles).astype(jnp.int32)
            sources = jnp.take(pieces, picked, axis=0)
            live_mask = (slot_ids < tile_counts[row_num, rep_num]).astype(jnp.float32)
            product = jnp.einsum("tij,tjf->tif", adjacency_tiles[row_num, rep_num], sources, precision=lax.Precision.HIGHEST)
            product = product * live_mask[:, None, None]
            placing = (tile_rows[row_num, rep_num][None, :] == lane_ids[:, None]).astype(jnp.float32)
            added = jnp.dot(placing, product.reshape(TMAX, TILE * F), precision=lax.Precision.HIGHEST)
            return running + added, None

        start = jnp.zeros((row_tiles, TILE * F), jnp.float32)
        running, unused = lax.scan(one_rep, start, jnp.arange(N_REP, dtype=jnp.int32))
        return running.reshape(VB, F)

    return lax.map(one_row, jnp.arange(N_ROW, dtype=jnp.int32)).reshape(NV, F)


def reference(features, adjacency_tiles, tile_rows, tile_cols, tile_counts, plan, weights):
    hidden = features
    for layer_num in range(LAYERS):
        aggregated = spread(hidden, adjacency_tiles, tile_rows, tile_cols, tile_counts, plan)
        hidden = jnp.maximum(jnp.dot(aggregated, weights[layer_num], precision=lax.Precision.HIGHEST), 0.0)
    return hidden
```

```python
import functools
import math

import jax
import jax.numpy as jnp
from jax import lax
from jax.experimental import pallas as pl
from jax.experimental.pallas import tpu as pltpu
from jax.sharding import PartitionSpec as P


def power_of_two(n):
    return n & (n - 1) == 0


def exchange(x, axis, n):
    if not power_of_two(n):
        return lax.all_to_all(x, axis, 0, 0)
    me = lax.axis_index(axis)
    out = x
    for mask in range(1, n):
        piece = lax.dynamic_index_in_dim(x, me ^ mask, 0, keepdims=True)
        came = lax.ppermute(piece, axis, [(i, i ^ mask) for i in range(n)])
        out = lax.dynamic_update_slice_in_dim(out, came, me ^ mask, 0)
    return out


def gather_pieces(x, axis, n):
    def send(value, mask):
        return lax.ppermute(value, axis, [(i, i ^ mask) for i in range(n)])

    pieces = [(0, 0, x)]
    if n == 8:
        half = x.shape[0] // 2
        left = send(x, 2)
        right = send(x, 4)
        pieces.append((2, 0, left))
        pieces.append((4, 0, right))
        pieces.append((6, 0, send(right[:half], 2)))
        pieces.append((6, half, send(left[half:], 4)))
    else:
        for mask in range(2, n, 2):
            pieces.append((mask, 0, send(x, mask)))
    return pieces + [(mask | 1, first, send(value, 1)) for mask, first, value in pieces]


def split(value):
    high = value.astype(jnp.bfloat16)
    low = (value - high.astype(jnp.float32)).astype(jnp.bfloat16)
    return high, low


def tile_kernel(places, sections, chunk_tiles, place_ref, rows_ref, cols_ref, tiles_ref, *rest):
    pieces = rest[: len(places)]
    out_ref, tiles, high, low, sems = rest[len(places) :]
    slots, edge, _ = tiles.shape
    count = place_ref[1]
    me = place_ref[0]
    chunks = slots // chunk_tiles

    def chunk_copy(index):
        window = pl.ds(index * chunk_tiles, chunk_tiles)
        return pltpu.make_async_copy(tiles_ref.at[window], tiles.at[window], sems.at[index])

    used = pl.cdiv(count, chunk_tiles)

    @pl.loop(0, used)
    def _(index):
        chunk_copy(index).start()

    out_ref[...] = jnp.zeros_like(out_ref)
    block_len = out_ref.shape[0]
    reps, run = places[0][2], places[0][3]
    for (mask, first, _, _), piece in zip(places, pieces):
        owner = me ^ mask
        for at in range(0, piece.shape[0], run):
            source = (first + at) // run
            rep, section = source // sections, source % sections
            base = section * block_len + rep * (block_len // reps)
            row = pl.multiple_of(base + owner * run, run)
            column = row // edge
            inner = pl.multiple_of(row % edge, run)
            h, l = split(piece[pl.ds(at, run), :])
            high[column, pl.ds(inner, run), :] = h
            high[column, pl.ds(edge + inner, run), :] = h
            low[column, pl.ds(inner, run), :] = l

    def add_tile(slot):
        row = pl.multiple_of(rows_ref[slot] * edge, edge)
        column = cols_ref[slot]
        h, l = split(tiles[slot])
        product = jnp.dot(
            jnp.concatenate([h, l], axis=1), high[column], preferred_element_type=jnp.float32
        )
        product += jnp.dot(h, low[column], preferred_element_type=jnp.float32)
        out_ref[pl.ds(row, edge), :] += product

    whole = count // chunk_tiles

    @pl.loop(0, whole)
    def _(index):
        chunk_copy(index).wait()
        for step in range(chunk_tiles):
            add_tile(index * chunk_tiles + step)

    @pl.when(whole < used)
    def _():
        chunk_copy(whole).wait()

        @pl.loop(whole * chunk_tiles, count)
        def _(slot):
            add_tile(slot)


def tile_sum(pieces, reps, sections, run, tiles, rows, cols, count, block_len):
    slots, edge, _ = tiles.shape
    width = pieces[0][2].shape[1]
    chunk_tiles = math.gcd(slots, 8)
    places = [(mask, first, reps, run) for mask, first, _ in pieces]
    columns = sections * block_len // edge
    scalar = jnp.stack([lax.axis_index("row").astype(jnp.int32), count])
    return pl.pallas_call(
        functools.partial(tile_kernel, places, sections, chunk_tiles),
        out_shape=jax.ShapeDtypeStruct((block_len, width), jnp.float32),
        in_specs=[pl.BlockSpec(memory_space=pltpu.SMEM)] * 3
        + [pl.BlockSpec(memory_space=pl.ANY)]
        + [pl.BlockSpec(memory_space=pltpu.VMEM)] * len(pieces),
        out_specs=pl.BlockSpec(memory_space=pltpu.VMEM),
        scratch_shapes=[
            pltpu.VMEM((slots, edge, edge), jnp.float32),
            pltpu.VMEM((columns, 2 * edge, width), jnp.bfloat16),
            pltpu.VMEM((columns, edge, width), jnp.bfloat16),
            pltpu.SemaphoreType.DMA((slots // chunk_tiles,)),
        ],
    )(scalar, rows, cols, tiles, *[value for _, _, value in pieces])


def shards(n_row, n_rep, features, adjacency_tiles, tile_rows, tile_cols, tile_counts, plan, weights):
    block_len, width = features.shape
    sections = plan.shape[1]
    share_len = block_len // n_rep
    run = share_len // n_row
    tiles, rows, cols = adjacency_tiles[0, 0], tile_rows[0, 0], tile_cols[0, 0]
    count = tile_counts[0, 0]
    share = lax.dynamic_slice_in_dim(features, lax.axis_index("rep") * share_len, share_len, 0)
    for layer in range(weights.shape[0]):
        by_block = exchange(share.reshape(n_row, run, width), "row", n_row)
        wanted = jnp.take(by_block, plan.reshape(-1), axis=0)
        wanted = wanted.reshape(n_rep, sections * run, width)
        mine = exchange(wanted, "rep", n_rep).reshape(n_rep * sections * run, width)
        pieces = gather_pieces(mine, "row", n_row)
        partial = tile_sum(pieces, n_rep, sections, run, tiles, rows, cols, count, block_len)
        total = lax.psum_scatter(partial, "rep", scatter_dimension=0, tiled=True)
        share = jnp.maximum(
            jnp.dot(total, weights[layer], precision=lax.Precision.HIGHEST), 0.0
        )
    return share


def solution(mesh):
    return jax.shard_map(
        functools.partial(shards, mesh.shape["row"], mesh.shape["rep"]),
        mesh=mesh,
        in_specs=(
            P("row", None),
            P("row", "rep", None, None, None),
            P("row", "rep", None),
            P("row", "rep", None),
            P("row", "rep"),
            P(),
            P(),
        ),
        out_specs=P(("row", "rep"), None),
        check_vma=False,
    )
```

```python
import functools
import math

import jax
import jax.numpy as jnp
from jax import lax
from jax.experimental import pallas as pl
from jax.experimental.pallas import tpu as pltpu
from jax.sharding import PartitionSpec as P

GROUP = 8
AHEAD = 6


def send(value, axis, n, mask):
    return lax.ppermute(value, axis, [(i, i ^ mask) for i in range(n)])


def exchange(pieces, axis, n):
    pieces = lax.optimization_barrier(tuple(pieces))
    return [pieces[0]] + [send(pieces[mask], axis, n, mask) for mask in range(1, n)]


def gather_pieces(x, axis, n):
    pieces = [(0, 0, x)]
    if n == 8:
        half = x.shape[0] // 2
        left = send(x, axis, n, 2)
        right = send(x, axis, n, 4)
        pieces.append((2, 0, left))
        pieces.append((4, 0, right))
        pieces.append((6, 0, send(right[:half], axis, n, 2)))
        pieces.append((6, half, send(left[half:], axis, n, 4)))
    else:
        for mask in range(2, n, 2):
            pieces.append((mask, 0, send(x, axis, n, mask)))
    return pieces + [(mask | 1, first, send(value, axis, n, 1)) for mask, first, value in pieces]


def split(value):
    high = value.astype(jnp.bfloat16)
    low = (value - high.astype(jnp.float32)).astype(jnp.bfloat16)
    return high, low


class Layout:
    def __init__(self, block_len, width, edge, n_row, n_rep, sections):
        self.block_len, self.width, self.edge = block_len, width, edge
        self.n_row, self.n_rep, self.sections = n_row, n_rep, sections
        self.share_len = block_len // n_rep
        self.share_tiles = self.share_len // edge
        fits = self.share_tiles % 2 == 0 and self.share_len // (2 * n_row) % 16 == 0
        self.chunks = 2 if fits else 1
        self.chunk_len = self.share_len // self.chunks
        self.chunk_tiles = self.share_tiles // self.chunks
        self.run = self.chunk_len // n_row
        self.columns = sections * n_rep * self.chunk_tiles


def sort_kernel(lay, rows_ref, cols_ref, count_ref, slot_ref, dest_ref, col_ref, bound_ref):
    count = count_ref[0]
    row_tiles = lay.block_len // lay.edge

    def place(tile):
        rep, inner = tile // lay.share_tiles, tile % lay.share_tiles
        return rep, inner // lay.chunk_tiles, inner % lay.chunk_tiles

    def step(slot, carry):
        low, high = carry
        rep, chunk, inner = place(rows_ref[slot])
        dest = chunk * (lay.block_len // lay.chunks) + (rep * lay.chunk_tiles + inner) * lay.edge
        section, tile = cols_ref[slot] // row_tiles, cols_ref[slot] % row_tiles
        rep, chunk, inner = place(tile)
        position = jnp.where(chunk == 0, low, high)
        slot_ref[position] = slot
        dest_ref[position] = dest
        col_ref[position] = (section * lay.n_rep + rep) * lay.chunk_tiles + inner
        first = jnp.where(chunk == 0, 1, 0)
        return low + first, high - (1 - first)

    low, _ = lax.fori_loop(0, count, step, (jnp.int32(0), count - 1))
    bound_ref[0] = 0
    bound_ref[1] = low
    bound_ref[2] = count


def sort_tiles(lay, rows, cols, count):
    slots = rows.shape[0]
    smem = pl.BlockSpec(memory_space=pltpu.SMEM)
    ints = jax.ShapeDtypeStruct((slots,), jnp.int32)
    return pl.pallas_call(
        functools.partial(sort_kernel, lay),
        out_shape=[ints, ints, ints, jax.ShapeDtypeStruct((3,), jnp.int32)],
        in_specs=[smem] * 3,
        out_specs=[smem] * 4,
        name="sort_tiles",
    )(rows, cols, count)


def tile_kernel(lay, chunk, places, prior, *refs):
    slot_ref, dest_ref, col_ref, bound_ref, me_ref, tiles_ref = refs[:6]
    pieces = refs[6 : 6 + len(places)]
    refs = refs[6 + len(places) :]
    if prior:
        prior_ref, refs = refs[0], refs[1:]
    out_ref, acc, tiles, high, low, sems, edge_sem = refs
    edge, run = lay.edge, lay.run
    start = bound_ref[chunk]
    stop = bound_ref[chunk + 1] if lay.chunks > 1 else bound_ref[2]
    groups = pl.cdiv(stop - start, GROUP)
    block = acc.at[pl.ds(0, lay.block_len)]

    def fetch(group):
        for step in range(GROUP):
            position = jnp.minimum(start + group * GROUP + step, stop - 1)
            pltpu.make_async_copy(
                tiles_ref.at[slot_ref[position]], tiles.at[group * GROUP + step], sems.at[group]
            ).start()

    for group in range(AHEAD):
        pl.when(group < groups)(functools.partial(fetch, group))

    if prior:
        first_copy = pltpu.make_async_copy(prior_ref, block, edge_sem)
        first_copy.start()
    else:
        acc[...] = jnp.zeros_like(acc)

    me_row, me_rep = me_ref[0], me_ref[1]
    for (mask, first), piece in zip(places, pieces):
        owner = me_row ^ mask
        for at in range(0, piece.shape[0], run):
            source = (first + at) // run
            rep, section = me_rep ^ (source // lay.sections), source % lay.sections
            row = owner * run
            column = (section * lay.n_rep + rep) * lay.chunk_tiles + row // edge
            inner = pl.multiple_of(row % edge, run)
            h, l = split(piece[pl.ds(at, run), :])
            high[column, pl.ds(inner, run), :] = h
            high[column, pl.ds(edge + inner, run), :] = h
            low[column, pl.ds(inner, run), :] = l
    if prior:
        first_copy.wait()

    @pl.loop(0, groups)
    def _(group):
        pl.when(group + AHEAD < groups)(lambda: fetch(group + AHEAD))
        window = pl.ds(group * GROUP, GROUP)
        pltpu.make_async_copy(
            tiles_ref.at[pl.ds(0, GROUP)], tiles.at[window], sems.at[group]
        ).wait()
        for step in range(GROUP):
            position = start + group * GROUP + step
            live = position < stop
            position = jnp.minimum(position, stop - 1)
            row = jnp.where(live, dest_ref[position], lay.block_len)
            row = pl.multiple_of(row, edge)
            column = col_ref[position]
            h, l = split(tiles[group * GROUP + step])
            product = jnp.dot(
                jnp.concatenate([h, l], axis=1),
                high[column],
                preferred_element_type=jnp.float32,
            )
            product += jnp.dot(h, low[column], preferred_element_type=jnp.float32)
            acc[pl.ds(row, edge), :] += product

    last_copy = pltpu.make_async_copy(block, out_ref, edge_sem)
    last_copy.start()
    last_copy.wait()


def tile_sum(lay, chunk, lists, me, tiles, pieces, prior):
    slots, edge, _ = tiles.shape
    places = [(mask, first) for mask, first, _ in pieces]
    smem = pl.BlockSpec(memory_space=pltpu.SMEM)
    anywhere = pl.BlockSpec(memory_space=pl.ANY)
    before = [] if prior is None else [prior]
    padded = -(-slots // GROUP) * GROUP
    return pl.pallas_call(
        functools.partial(tile_kernel, lay, chunk, places, prior is not None),
        out_shape=jax.ShapeDtypeStruct((lay.block_len, lay.width), jnp.float32),
        in_specs=[smem] * 5
        + [anywhere]
        + [pl.BlockSpec(memory_space=pltpu.VMEM)] * len(pieces)
        + [anywhere] * len(before),
        out_specs=anywhere,
        scratch_shapes=[
            pltpu.VMEM((lay.block_len + edge, lay.width), jnp.float32),
            pltpu.VMEM((padded, edge, edge), jnp.float32),
            pltpu.VMEM((lay.columns, 2 * edge, lay.width), jnp.bfloat16),
            pltpu.VMEM((lay.columns, edge, lay.width), jnp.bfloat16),
            pltpu.SemaphoreType.DMA((padded // GROUP,)),
            pltpu.SemaphoreType.DMA,
        ],
        name="tile_sum",
    )(*lists, me, tiles, *[value for _, _, value in pieces], *before)


def shards(n_row, n_rep, features, adjacency_tiles, tile_rows, tile_cols, tile_counts, plan, weights):
    block_len, width = features.shape
    tiles = adjacency_tiles[0, 0]
    lay = Layout(block_len, width, tiles.shape[1], n_row, n_rep, plan.shape[1])
    lists = sort_tiles(lay, tile_rows[0, 0], tile_cols[0, 0], tile_counts[0])
    me_row = lax.axis_index("row").astype(jnp.int32)
    me_rep = lax.axis_index("rep").astype(jnp.int32)
    me = jnp.stack([me_row, me_rep])
    blocks = plan.reshape(-1)

    def rows_at(x, start, length):
        return lax.dynamic_slice_in_dim(x, start, length, 0)

    shares = [
        rows_at(features, me_rep * lay.share_len + chunk * lay.chunk_len, lay.chunk_len)
        for chunk in range(lay.chunks)
    ]
    for layer in range(weights.shape[0]):
        gathered = []
        for chunk in range(lay.chunks):
            by_row = exchange(
                [rows_at(shares[chunk], (me_row ^ mask) * lay.run, lay.run) for mask in range(n_row)],
                "row",
                n_row,
            )
            by_row = jnp.concatenate(by_row, 0)
            wanted = []
            for mask in range(n_rep):
                picked = [
                    rows_at(
                        by_row,
                        (me_row ^ blocks[(me_rep ^ mask) * lay.sections + section]) * lay.run,
                        lay.run,
                    )
                    for section in range(lay.sections)
                ]
                wanted.append(jnp.concatenate(picked, 0))
            mine = jnp.concatenate(exchange(wanted, "rep", n_rep), 0)
            gathered.append(gather_pieces(mine, "row", n_row))
        partial = None
        for chunk in range(lay.chunks):
            partial = tile_sum(lay, chunk, lists, me, tiles, gathered[chunk], partial)
        size = block_len // lay.chunks
        shares = []
        for chunk in range(lay.chunks):
            part = lax.slice_in_dim(partial, chunk * size, (chunk + 1) * size)
            total = lax.psum_scatter(part, "rep", scatter_dimension=0, tiled=True)
            product = jnp.dot(total, weights[layer], precision=lax.Precision.HIGH)
            shares.append(jnp.maximum(product, 0.0))
    return jnp.concatenate(shares, 0)


def solution(mesh):
    return jax.shard_map(
        functools.partial(shards, mesh.shape["row"], mesh.shape["rep"]),
        mesh=mesh,
        in_specs=(
            P("row", None),
            P("row", "rep", None, None, None),
            P("row", "rep", None),
            P("row", "rep", None),
            P("row", "rep"),
            P(),
            P(),
        ),
        out_specs=P(("row", "rep"), None),
        check_vma=False,
    )
```

```python
import functools
import math

import jax
import jax.numpy as jnp
from jax import lax
from jax.experimental import pallas as pl
from jax.experimental.pallas import tpu as pltpu
from jax.sharding import PartitionSpec as P


def send(value, axis, n, mask):
    return lax.ppermute(value, axis, [(i, i ^ mask) for i in range(n)])


def exchange(pieces, axis, n):
    pieces = lax.optimization_barrier(tuple(pieces))
    came = {mask: send(pieces[mask], axis, n, mask) for mask in reversed(range(1, n))}
    return [pieces[0]] + [came[mask] for mask in range(1, n)]


def exchange_by_chip(pieces, axis, n):
    same = jnp.concatenate(pieces[0::2], 0)
    other = send(jnp.concatenate(pieces[1::2], 0), axis, n, 1)
    length = pieces[0].shape[0]
    pairs = [
        jnp.concatenate([x[at * length : (at + 1) * length] for x in (same, other)], 0)
        for at in range(n // 2)
    ]
    pairs = lax.optimization_barrier(tuple(pairs))
    return [pairs[0]] + [send(pairs[at], axis, n, 2 * at) for at in range(1, n // 2)]


def gather_pieces(x, axis, n):
    pieces = [(0, 0, x)]
    if n == 8:
        half = x.shape[0] // 2
        left = send(x, axis, n, 2)
        right = send(x, axis, n, 4)
        pieces.append((2, 0, left))
        pieces.append((4, 0, right))
        pieces.append((6, 0, send(right[:half], axis, n, 2)))
        pieces.append((6, half, send(left[half:], axis, n, 4)))
    else:
        for mask in range(2, n, 2):
            pieces.append((mask, 0, send(x, axis, n, mask)))
    return pieces + [(mask | 1, first, send(value, axis, n, 1)) for mask, first, value in pieces]


def scatter_sum(partial, axis, n, me):
    if n != 4:
        return lax.psum_scatter(partial, axis, scatter_dimension=0, tiled=True)
    size = partial.shape[0] // n

    def share(lower, upper):
        index = jnp.where(me < n // 2, lower, upper)
        return lax.dynamic_slice_in_dim(partial, index * size, size, 0)

    def shift(value, pairs):
        return lax.ppermute(value, axis, pairs)

    inward, across, outward = [(0, 1), (3, 2)], [(1, 2), (2, 1)], [(2, 3), (1, 0)]
    first = [share(3, 0), share(2, 1), share(1, 2)]
    far, middle, near = lax.optimization_barrier(tuple(first))
    far = shift(far, inward)
    middle = shift(middle, inward)
    near = shift(near, inward)
    far = shift(share(3, 0) + far, across)
    middle = shift(share(2, 1) + middle, across)
    far = shift(share(0, 3) + far, outward)
    own = lax.dynamic_slice_in_dim(partial, me * size, size, 0)
    return (own + near) + (middle + far)


def split(value):
    high = value.astype(jnp.bfloat16)
    low = (value - high.astype(jnp.float32)).astype(jnp.bfloat16)
    return high, low


def tile_kernel(places, n_rep, sections, run, chunk_tiles, me_ref, count_ref, rows_ref, cols_ref, tiles_ref, *rest):
    pieces = rest[: len(places)]
    out_ref, tiles, high, low, sems = rest[len(places) :]
    slots, edge, _ = tiles.shape
    count = count_ref[0]
    me_row, me_rep = me_ref[0], me_ref[1]

    def chunk_copy(index):
        window = pl.ds(index * chunk_tiles, chunk_tiles)
        return pltpu.make_async_copy(tiles_ref.at[window], tiles.at[window], sems.at[index])

    used = pl.cdiv(count, chunk_tiles)

    @pl.loop(0, used)
    def _(index):
        chunk_copy(index).start()

    out_ref[...] = jnp.zeros_like(out_ref)
    block_len = out_ref.shape[0]
    for (mask, first), piece in zip(places, pieces):
        owner = me_row ^ mask
        for at in range(0, piece.shape[0], run):
            source = (first + at) // run
            rep, section = me_rep ^ (source // sections), source % sections
            row = section * block_len + rep * (block_len // n_rep) + owner * run
            row = pl.multiple_of(row, run)
            column = row // edge
            inner = pl.multiple_of(row % edge, run)
            h, l = split(piece[pl.ds(at, run), :])
            high[column, pl.ds(inner, run), :] = h
            high[column, pl.ds(edge + inner, run), :] = h
            low[column, pl.ds(inner, run), :] = l

    def add_tile(slot):
        row = pl.multiple_of(rows_ref[slot] * edge, edge)
        column = cols_ref[slot]
        h, l = split(tiles[slot])
        product = jnp.dot(
            jnp.concatenate([h, l], axis=1), high[column], preferred_element_type=jnp.float32
        )
        product += jnp.dot(h, low[column], preferred_element_type=jnp.float32)
        out_ref[pl.ds(row, edge), :] += product

    whole = count // chunk_tiles

    @pl.loop(0, whole)
    def _(index):
        chunk_copy(index).wait()
        for step in range(chunk_tiles):
            add_tile(index * chunk_tiles + step)

    @pl.when(whole < used)
    def _():
        chunk_copy(whole).wait()

        @pl.loop(whole * chunk_tiles, count)
        def _(slot):
            add_tile(slot)


def tile_sum(pieces, n_rep, sections, run, me, count, rows, cols, tiles, block_len):
    slots, edge, _ = tiles.shape
    width = pieces[0][2].shape[1]
    chunk_tiles = math.gcd(slots, 8)
    places = [(mask, first) for mask, first, _ in pieces]
    columns = sections * block_len // edge
    return pl.pallas_call(
        functools.partial(tile_kernel, places, n_rep, sections, run, chunk_tiles),
        out_shape=jax.ShapeDtypeStruct((block_len, width), jnp.float32),
        in_specs=[pl.BlockSpec(memory_space=pltpu.SMEM)] * 4
        + [pl.BlockSpec(memory_space=pl.ANY)]
        + [pl.BlockSpec(memory_space=pltpu.VMEM)] * len(pieces),
        out_specs=pl.BlockSpec(memory_space=pltpu.VMEM),
        scratch_shapes=[
            pltpu.VMEM((slots, edge, edge), jnp.float32),
            pltpu.VMEM((columns, 2 * edge, width), jnp.bfloat16),
            pltpu.VMEM((columns, edge, width), jnp.bfloat16),
            pltpu.SemaphoreType.DMA((slots // chunk_tiles,)),
        ],
        name="tile_sum",
    )(me, count, rows, cols, tiles, *[value for _, _, value in pieces])


def shards(n_row, n_rep, features, adjacency_tiles, tile_rows, tile_cols, tile_counts, plan, weights):
    block_len, _ = features.shape
    sections = plan.shape[1]
    share_len = block_len // n_rep
    run = share_len // n_row
    tiles, rows, cols = adjacency_tiles[0, 0], tile_rows[0, 0], tile_cols[0, 0]
    count = tile_counts[0]
    me_row = lax.axis_index("row").astype(jnp.int32)
    me_rep = lax.axis_index("rep").astype(jnp.int32)
    me = jnp.stack([me_row, me_rep])
    blocks = plan.reshape(-1)

    def rows_at(x, start, length):
        return lax.dynamic_slice_in_dim(x, start, length, 0)

    share = rows_at(features, me_rep * share_len, share_len)
    for layer in range(weights.shape[0]):
        by_row = [rows_at(share, (me_row ^ mask) * run, run) for mask in range(n_row)]
        by_row = jnp.concatenate(exchange_by_chip(by_row, "row", n_row), 0)
        wanted = []
        for mask in range(n_rep):
            first = (me_rep ^ mask) * sections
            picked = [
                rows_at(by_row, (me_row ^ blocks[first + section]) * run, run)
                for section in range(sections)
            ]
            wanted.append(jnp.concatenate(picked, 0))
        mine = jnp.concatenate(exchange(wanted, "rep", n_rep), 0)
        pieces = gather_pieces(mine, "row", n_row)
        partial = tile_sum(pieces, n_rep, sections, run, me, count, rows, cols, tiles, block_len)
        total = scatter_sum(partial, "rep", n_rep, me_rep)
        product = jnp.dot(total, weights[layer], precision=lax.Precision.HIGH)
        share = jnp.maximum(product, 0.0)
    return share


def solution(mesh):
    return jax.shard_map(
        functools.partial(shards, mesh.shape["row"], mesh.shape["rep"]),
        mesh=mesh,
        in_specs=(
            P("row", None),
            P("row", "rep", None, None, None),
            P("row", "rep", None),
            P("row", "rep", None),
            P("row", "rep"),
            P(),
            P(),
        ),
        out_specs=P(("row", "rep"), None),
        check_vma=False,
    )
```
